128 devices in a mesh: own: 8 (over y_lo, x), dp: 16 (over y_hi, z, core).
Axes of the slice: x: 4, y: 4 (y_hi: 2, y_lo: 2; y = y_hi * 2 + y_lo), z: 4, core: 2. Of those that a mesh axis runs over, the one named last changes fastest.
Arguments:
- tokens: bfloat16 [16384, 1536], P('dp'), may hold values from -6 to 6
- assign: int32 [128, 2], P('dp'), may hold values from 0 to 7, all different within a row; in each aligned block of 8 rows (0 to 7, 8 to 15, ...) at most 5 rows name the same one
- gates: float32 [16384, 2], P('dp'), may hold values from 0.25 to 1
- cot: bfloat16 [16384, 1536], P('dp', 'own'), may hold values from -1.75 to 1.75
- w_in: bfloat16 [8, 1536, 2048], P('own', None, 'dp'), may hold values from -0.15625 to 0.15625
- w_out: bfloat16 [8, 2048, 1536], P('own', 'dp'), may hold values from -0.125 to 0.125
Outputs:
- mixed: bfloat16 [16384, 1536], P('dp', 'own')
- grad_tokens: bfloat16 [16384, 1536], P('dp', 'own')
- grad_w_in: float32 [8, 1536, 2048], P('own', None, 'dp')
- grad_w_out: float32 [8, 2048, 1536], P('own', 'dp')
The draws below stay inside these ranges and needn't reach their ends.
Inputs may be any that keep to these rules, and one draw needn't show every extreme that they name: `assign`: the two entries of a block name different experts. Among the 8 blocks of one index of dp no expert is named more than 5 times, and in every draw some expert is named exactly 5 times by the blocks of some index of dp.
All inputs are finite; a program needn't handle non-finite values.
Results may differ from the reference program's by a relative error of at most 0.012.
Values may be sent and summed in bfloat16 or wider, within the bound.
No kernel may reach another device: no remote copies, remote signals or barrier semaphores. Data moves between devices by JAX's collectives and lax.ppermute only.
A program may use at most 128 MiB of HBM per device.

```python
import math
import jax
import jax.numpy as jnp
import numpy as np
from jax import lax

D = 1536
FF = 2048
EXPERTS = 8
BLOCK = 128
BLK_DEV = 8
CAP = 5
BLOCKS = 128
TOKENS = 16384
N_OWN = 8
N_DP = 16


def levels(key, shape, cuts, smallest, largest):
    gain, own = 1.0, jax.random.fold_in(key, 6)
    for position, shards_of in cuts:
        heights = jnp.exp(jax.random.uniform(jax.random.fold_in(own, position), (shards_of,), jnp.float32, smallest / len(cuts), largest / len(cuts)))
        gain = gain * jnp.repeat(heights, shape[position] // shards_of).reshape([-1 if axis == position else 1 for axis in range(len(shape))])
    return gain


def shared_out(key, own, number, rows, count, top, reach, lean):
    sequence = jax.random.permutation(key, count)
    packed, ordinary = portions_of(count, rows * top, reach, lean, True), portions_of(count, rows * top, reach, lean, False)
    places = jnp.arange(count)

    def named(sizes, rotation):
        used = int((sizes > 0).sum())
        fixed = max(1, used // 4)
        shifted = fixed + (places - fixed + rotation * (used - fixed)) % max(1, count - fixed)
        return jnp.zeros((count,), jnp.int32).at[sequence[jnp.where(places < fixed, places, shifted)]].set(jnp.asarray(sizes, jnp.int32))

    sizes = jnp.where(number % 4 == 0, named(packed, number // 4), named(ordinary, number - number // 4 - 1))
    mixed = jax.random.permutation(jax.random.fold_in(own, 3), count)
    source_of, sink = mixed[0:count // 2 * 2:2], mixed[1:count // 2 * 2:2]
    room = jnp.minimum(sizes[source_of] - 1, reach - sizes[sink]) // 2
    room = jnp.where((source_of == sequence[0]) | (sink == sequence[0]) | (sizes[sink] == 0), 0, jnp.maximum(room, 0))
    shifted = jax.random.randint(jax.random.fold_in(own, 4), (count // 2,), 0, 1 << 20) % (room + 1)
    sizes = sizes.at[source_of].add(-shifted).at[sink].add(shifted)
    members = jnp.searchsorted(jnp.cumsum(sizes), jnp.arange(rows * top), side="right").astype(jnp.int32)
    table = members.reshape(top, rows).T
    table = table[jax.random.permutation(jax.random.fold_in(own, 1), rows)]
    rotation = jax.random.randint(jax.random.fold_in(own, 2), (rows, 1), 0, top)
    return jnp.take_along_axis(table, (jnp.arange(top)[None, :] + rotation) % top, axis=1)


def portions_of(amount, total, reach, lean, full):
    portions = [(1 << 20) // math.isqrt(standing ** lean) + 1 for standing in range(1, amount + 1)]
    largest = reach if full else min(reach, max(-(-total // amount), total * portions[0] // sum(portions)))
    least = 1 if total - largest >= amount - 1 else 0
    given, rest = [largest] + [least] * (amount - 1), total - largest - least * (amount - 1)
    while rest > 0:
        candidates = [i for i in range(1, amount) if given[i] < largest] or [i for i in range(1, amount) if given[i] < reach]
        pool, budget = sum([portions[i] for i in candidates]), rest
        for i in candidates:
            more = min(reach - given[i], max(1, budget * portions[i] // pool), rest)
            given[i] = given[i] + more
            rest = rest - more
    return np.array(given)


def centred(own_key, extent, deviation, limit, cuts=(), kind=jnp.bfloat16):
    gain = levels(own_key, extent, cuts, -0.22, 0.18) if cuts else 1.0
    array = jax.random.normal(own_key, extent, jnp.float32) * deviation * gain
    return jnp.minimum(jnp.maximum(array, -limit), limit).astype(kind)


def setup_inputs(seed: int = 0) -> dict:
    seeds = jax.random.split(jax.random.key(seed), 7)
    tokens = centred(seeds[0], (TOKENS, D), 1.0, 6.0, ((0, 16),))
    assign_keys = jax.random.split(jax.random.fold_in(seeds[1], 1), BLOCKS // BLK_DEV)
    assign_turns = jax.random.permutation(jax.random.fold_in(seeds[1], 3), BLOCKS // BLK_DEV)
    assign = jax.vmap(lambda own, number: shared_out(jax.random.fold_in(seeds[1], 2), own, number, BLK_DEV, EXPERTS, 2, CAP, 2))(assign_keys, assign_turns).reshape((BLOCKS, 2))
    gates = jnp.clip(0.25 + 0.75 * jax.random.uniform(seeds[2], (TOKENS, 2), jnp.float32) ** levels(seeds[2], (TOKENS, 2), ((0, 16),), -0.2, 0.2), 0.25, 1.0)
    cot = centred(seeds[3], (TOKENS, D), 0.3, 1.75, ((0, 16), (1, 8)))
    w_in = centred(seeds[4], (EXPERTS, D, FF), D ** -0.5, 0.15625, ((0, 8), (2, 16)))
    w_out = centred(seeds[5], (EXPERTS, FF, D), FF ** -0.5, 0.125, ((0, 8), (1, 16)))
    return {"tokens": tokens, "assign": assign, "gates": gates, "cot": cot, "w_in": w_in, "w_out": w_out}


def pick_blocks(assign_rows, expert, capacity):
    hit_flag = jnp.logical_or(assign_rows[:, 0] == expert, assign_rows[:, 1] == expert).astype(jnp.int32)
    slot_rank = jnp.cumsum(hit_flag) - 1
    slot_ids = jnp.arange(capacity, dtype=jnp.int32)
    matches = jnp.logical_and(hit_flag[None, :] == 1, slot_rank[None, :] == slot_ids[:, None]).astype(jnp.int32)
    where_idx = jnp.arange(assign_rows.shape[0], dtype=jnp.int32)
    blocks = jnp.sum(matches * where_idx[None, :], axis=1).astype(jnp.int32)
    is_valid = jnp.sum(matches, axis=1).astype(jnp.float32)
    return blocks, is_valid


def block_gates(assign_rows, gate_blocks, blocks, is_valid, expert):
    chosen = assign_rows[blocks]
    picked_gates = gate_blocks[blocks]
    first_hit = (chosen[:, 0] == expert).astype(jnp.float32)
    second_hit = (chosen[:, 1] == expert).astype(jnp.float32)
    mixing = picked_gates[..., 0] * first_hit[:, None] + picked_gates[..., 1] * second_hit[:, None]
    return mixing * is_valid[:, None]


def gelu_cdf(values):
    return 0.5 * (1.0 + jax.scipy.special.erf(values * 0.7071067811865476))


def gelu_slope(values):
    return gelu_cdf(values) + values * jnp.exp(-0.5 * values * values) * 0.3989422804014327


def place_rows(terms, blocks, block_count):
    block_len = terms.shape[-2]
    width = terms.shape[-1]
    zeros = jnp.zeros((block_count, block_len, width), jnp.float32)
    placed = zeros.at[blocks.reshape(-1)].add(terms.reshape(-1, block_len, width))
    return placed.reshape(block_count * block_len, width)


def owner_total(terms, blocks, block_count):
    own_count = EXPERTS // N_OWN
    grouped = terms.reshape((N_OWN, own_count * CAP) + terms.shape[2:])
    group_blocks = blocks.reshape(N_OWN, own_count * CAP)
    placed = jax.vmap(place_rows, (0, 0, None))(grouped, group_blocks, block_count)
    rounded = lax.optimization_barrier(placed.astype(jnp.bfloat16)).astype(jnp.float32)
    return jnp.sum(rounded, axis=0).astype(jnp.bfloat16)


def reference(tokens, assign, gates, cot, w_in, w_out):
    token_shards = tokens.reshape(N_DP, BLK_DEV, BLOCK, D)
    assign_shards = assign.reshape(N_DP, BLK_DEV, 2)
    gate_shards = gates.reshape(N_DP, BLK_DEV, BLOCK, 2)
    cot_shards = cot.reshape(N_DP, BLK_DEV, BLOCK, D)
    w_in32 = w_in.astype(jnp.float32)
    w_out32 = w_out.astype(jnp.float32)
    expert_ids = jnp.arange(EXPERTS, dtype=jnp.int32)

    def one_shard(carry, items):
        sum_in, sum_out = carry
        token_blocks, assign_rows, gate_blocks, cot_blocks = items
        blocks, is_valid = jax.vmap(pick_blocks, (None, 0, None))(assign_rows, expert_ids, CAP)
        mixing = jax.vmap(block_gates, (None, None, 0, 0, 0))(assign_rows, gate_blocks, blocks, is_valid, expert_ids)
        picked = token_blocks[blocks].reshape(EXPERTS, CAP * BLOCK, D)
        weight_rows = mixing.reshape(EXPERTS, CAP * BLOCK)
        pre_act = jnp.einsum('erd,edf->erf', picked.astype(jnp.float32), w_in32)
        hidden = (pre_act * gelu_cdf(pre_act)).astype(jnp.bfloat16)
        expert_out = jnp.einsum('erf,efd->erd', hidden.astype(jnp.float32), w_out32)
        contrib = (weight_rows[..., None] * expert_out).reshape(EXPERTS, CAP, BLOCK, D)
        mixed_rows = owner_total(contrib, blocks, BLK_DEV)
        cot_picked = cot_blocks[blocks].reshape(EXPERTS, CAP * BLOCK, D).astype(jnp.float32)
        grad_out = (weight_rows[..., None] * cot_picked).astype(jnp.bfloat16)
        grad_hidden = jnp.einsum('erd,efd->erf', grad_out.astype(jnp.float32), w_out32)
        grad_pre = (grad_hidden * gelu_slope(pre_act)).astype(jnp.bfloat16)
        grad_in_rows = jnp.einsum('erf,edf->erd', grad_pre.astype(jnp.float32), w_in32).reshape(EXPERTS, CAP, BLOCK, D)
        grad_rows = owner_total(grad_in_rows, blocks, BLK_DEV)
        out_part = jnp.einsum('erf,erd->efd', hidden.astype(jnp.float32), grad_out.astype(jnp.float32))
        in_part = jnp.einsum('erd,erf->edf', picked.astype(jnp.float32), grad_pre.astype(jnp.float32))
        out_part = lax.optimization_barrier(out_part.astype(jnp.bfloat16)).astype(jnp.float32)
        in_part = lax.optimization_barrier(in_part.astype(jnp.bfloat16)).astype(jnp.float32)
        return (sum_in + in_part, sum_out + out_part), (mixed_rows, grad_rows)

    start = (jnp.zeros((EXPERTS, D, FF), jnp.float32), jnp.zeros((EXPERTS, FF, D), jnp.float32))
    totals, rows = lax.scan(one_shard, start, (token_shards, assign_shards, gate_shards, cot_shards))
    mixed = rows[0].reshape(TOKENS, D)
    grad_tokens = rows[1].reshape(TOKENS, D)
    return mixed, grad_tokens, totals[0], totals[1]
```

```python
import jax
import jax.numpy as jnp
from jax import lax
from jax.sharding import Mesh, PartitionSpec as P

CAP = 5
BF = jnp.bfloat16
F32 = jnp.float32
OWN = ("y_lo", "x")
DP = ("y_hi", "z", "core")


def shift(value, axis, size, step):
    return lax.ppermute(value, axis, [(i, (i + step) % size) for i in range(size)])


def z_up(value):
    return shift(value, "z", 4, 1)


def z_down(value):
    return shift(value, "z", 4, 3)


def y_swap(value):
    return shift(value, "y_hi", 2, 1)


def core_swap(value):
    return shift(value, "core", 2, 1)


def z_gather(first, second):
    up_first, down_second = z_up(first), z_down(second)
    up_second, down_first = z_up(second), z_down(first)
    far_first, far_second = z_up(up_first), z_down(down_second)
    return (first, second), (up_first, up_second), (down_first, down_second), (far_first, far_second)


def gather_weights(block, axis):
    half = block.shape[0] // 2
    first, second = block[:half], block[half:]
    other_first, other_second = y_swap(first), y_swap(second)
    mine = z_gather(first, second)
    other = z_gather(other_first, other_second)
    return [
        jnp.concatenate([jnp.concatenate(m, 0), jnp.concatenate(o, 0)], axis)
        for m, o in zip(mine, other)
    ]


def scatter_sum(term_of, rows):
    far = term_of(3).astype(BF)
    half = far.shape[1] // 2
    got_up = z_up(far[:, :half])
    got_down = z_down(far[:, half:])
    up, down = term_of(2), term_of(1)
    up = jnp.concatenate([up[:, :half] + got_up.astype(F32), up[:, half:]], 1)
    down = jnp.concatenate([down[:, :half], down[:, half:] + got_down.astype(F32)], 1)
    from_below = z_up(up.astype(BF))
    from_above = z_down(down.astype(BF))
    near = term_of(0) + from_below.astype(F32) + from_above.astype(F32)
    return near[:rows] + y_swap(near[rows:].astype(BF)).astype(F32)


def gelu_cdf(values):
    return 0.5 * (1.0 + lax.erf(values * 0.7071067811865476))


def gelu_slope(values):
    return gelu_cdf(values) + values * jnp.exp(-0.5 * values * values) * 0.3989422804014327


def dot(a, b, dims):
    return lax.dot_general(a, b, (dims, ((), ())), preferred_element_type=F32)


def body(tokens, assign, gates, cot, w_in, w_out):
    w_in, w_out = w_in[0], w_out[0]
    width, units = w_in.shape
    block_count = assign.shape[0]
    block_len = tokens.shape[0] // block_count
    expert = lax.axis_index(OWN).astype(jnp.int32)

    hit = jnp.logical_or(assign[:, 0] == expert, assign[:, 1] == expert)
    order = jnp.arange(block_count, dtype=jnp.int32)
    earlier = jnp.logical_and(order[None, :] < order[:, None], hit[None, :])
    rank = jnp.sum(earlier.astype(jnp.int32), axis=1)
    slots = jnp.arange(CAP, dtype=jnp.int32)
    match = jnp.logical_and(hit[None, :], rank[None, :] == slots[:, None])
    blocks = jnp.sum(jnp.where(match, order[None, :], 0), axis=1)
    gate_blocks = gates.reshape(block_count, block_len, 2)
    block_weight = jnp.where((assign[:, 0] == expert)[:, None], gate_blocks[..., 0], 0.0) + jnp.where(
        (assign[:, 1] == expert)[:, None], gate_blocks[..., 1], 0.0
    )
    slot_weight = jnp.sum(jnp.where(match[:, :, None], block_weight[None], 0.0), axis=1)
    slot_weight = slot_weight.reshape(CAP * block_len, 1)

    cot_full = lax.all_gather(cot.T, OWN, axis=0, tiled=True).T
    in_groups = gather_weights(w_in, 1)
    picked = tokens.reshape(block_count, block_len, width)[blocks].reshape(CAP * block_len, width)
    rows = jnp.concatenate([picked, core_swap(picked)], 0)
    full_in = jnp.concatenate(in_groups, 1)
    pre = dot(rows, full_in, ((1,), (0,)))
    hidden = (pre * gelu_cdf(pre)).astype(BF)

    out_groups = gather_weights(w_out, 0)
    cot_picked = cot_full.reshape(block_count, block_len, width)[blocks].reshape(CAP * block_len, width)
    grad_mine = (slot_weight * cot_picked.astype(F32)).astype(BF)
    grad_out = jnp.concatenate([grad_mine, core_swap(grad_mine)], 0)

    group = 2 * units

    def out_term(k):
        return dot(hidden[:, k * group : (k + 1) * group], grad_out, ((0,), (0,)))

    grad_w_out = scatter_sum(out_term, units)

    full_out = jnp.concatenate(out_groups, 0)
    half_rows = CAP * block_len

    def place(part):
        total = part[:half_rows] + core_swap(part[half_rows:].astype(BF)).astype(F32)
        return total.reshape(CAP, block_len, width)[jnp.minimum(rank, CAP - 1)]

    mixed_rows = place(dot(hidden, full_out, ((1,), (0,)))) * block_weight[..., None]
    mixed_rows = mixed_rows.astype(BF).reshape(-1, width)
    mixed = lax.psum_scatter(mixed_rows.T, OWN, scatter_dimension=0, tiled=True).T

    grad_hidden = dot(grad_out, full_out, ((1,), (1,)))
    grad_pre = (grad_hidden * gelu_slope(pre)).astype(BF)

    def in_term(k):
        return dot(grad_pre[:, k * group : (k + 1) * group], rows, ((0,), (0,)))

    grad_w_in = scatter_sum(in_term, units)
    grad_rows = jnp.where(hit[:, None, None], place(dot(grad_pre, full_in, ((1,), (1,)))), 0.0)
    grad_rows = grad_rows.astype(BF).reshape(-1, width)
    grad_tokens = lax.psum_scatter(grad_rows.T, OWN, scatter_dimension=0, tiled=True).T
    return mixed, grad_tokens, grad_w_in.T[None], grad_w_out[None]


def solution(mesh):
    split = Mesh(mesh.devices.reshape(2, 4, 2, 4, 2), OWN + DP)
    return jax.shard_map(
        body,
        mesh=split,
        in_specs=(
            P(DP, None),
            P(DP, None),
            P(DP, None),
            P(DP, OWN),
            P(OWN, None, DP),
            P(OWN, DP, None),
        ),
        out_specs=(P(DP, OWN), P(DP, OWN), P(OWN, None, DP), P(OWN, DP, None)),
        check_vma=False,
    )
```

```python
import functools

import jax
import jax.numpy as jnp
from jax import lax
from jax.experimental import pallas as pl
from jax.experimental.pallas import tpu as pltpu
from jax.sharding import Mesh, PartitionSpec as P


CAP = 5
BF = jnp.bfloat16
F32 = jnp.float32
OWN = ("y_lo", "x")
DP = ("y_hi", "z", "core")


def shift(value, axis, size, step):
    return lax.ppermute(value, axis, [(i, (i + step) % size) for i in range(size)])


def ring_up(value, ring):
    return shift(value, ring[0], 4, 1)


def ring_down(value, ring):
    return shift(value, ring[0], 4, 3)


def side_swap(value, ring):
    return shift(value, ring[1], 2, 1)


def core_swap(value):
    return shift(value, "core", 2, 1)


def y_step_down(value):
    at = [(y % 2) * 2 + y // 2 for y in range(4)]
    return lax.ppermute(value, ("y_lo", "y_hi"), [(at[y], at[(y + 3) % 4]) for y in range(4)])


def ring_gather(block, other, ring):
    below, above = ring_up(block, ring), ring_down(block, ring)
    other_below, other_above = ring_up(other, ring), ring_down(other, ring)
    far, other_far = ring_up(below, ring), ring_down(other_above, ring)
    return [block, other, below, other_below, above, other_above, far, other_far]


def plus(term, got):
    return (term.astype(F32) + got.astype(F32)).astype(BF)


def ring_scatter(near, down, up, far, ring):
    got_up = ring_up(far[0].astype(BF), ring)
    got_down = ring_down(far[1].astype(BF), ring)
    below_other = ring_up(up[1].astype(BF), ring)
    above_this = ring_down(down[0].astype(BF), ring)
    below_this = ring_up(plus(up[0], got_up), ring)
    above_other = ring_down(plus(down[1], got_down), ring)
    other = near[1].astype(F32) + below_other.astype(F32) + above_other.astype(F32)
    this = near[0].astype(F32) + below_this.astype(F32) + above_this.astype(F32)
    return this + side_swap(other.astype(BF), ring).astype(F32)


def gelu_cdf(values):
    return 0.5 * (1.0 + lax.erf(values * 0.7071067811865476))


def gelu_slope(values):
    return gelu_cdf(values) + values * jnp.exp(-0.5 * values * values) * 0.3989422804014327


def dot(a, b, dims):
    return lax.dot_general(a, b, (dims, ((), ())), preferred_element_type=F32)


def pick_kernel(blocks_ref, owners_ref, cot_ref, weight_ref, out_ref, whole_ref):
    del blocks_ref
    part = cot_ref.shape[0] // 8
    for position in range(8):
        at = pl.multiple_of(owners_ref[position] * part, part)
        whole_ref[pl.ds(at, part), :] = cot_ref[pl.ds(position * part, part), :]
    out_ref[...] = (whole_ref[...].T.astype(F32) * weight_ref[0]).astype(BF)


def pick_rows(cot_t, blocks, owners, slot_weight):
    width = cot_t.shape[0]
    cap, block_len, _ = slot_weight.shape
    return pl.pallas_call(
        pick_kernel,
        out_shape=jax.ShapeDtypeStruct((cap * block_len, width), BF),
        grid_spec=pltpu.PrefetchScalarGridSpec(
            num_scalar_prefetch=2,
            grid=(cap,),
            in_specs=[
                pl.BlockSpec((width, block_len), lambda k, b, o: (0, b[k])),
                pl.BlockSpec((1, block_len, 1), lambda k, b, o: (k, 0, 0)),
            ],
            out_specs=pl.BlockSpec((block_len, width), lambda k, b, o: (k, 0)),
            scratch_shapes=[pltpu.VMEM((width, block_len), BF)],
        ),
        cost_estimate=pl.CostEstimate(flops=2000000, bytes_accessed=8000000, transcendentals=0),
    )(blocks, owners, cot_t, slot_weight)


def place_kernel(slots_ref, owners_ref, mine_ref, theirs_ref, weight_ref, out_ref):
    part, block_len = out_ref.shape[0] // 8, weight_ref.shape[2]

    def one(block, carry):
        source = pl.ds(pl.multiple_of(slots_ref[block] * block_len, block_len), block_len)
        target = pl.ds(pl.multiple_of(block * block_len, block_len), block_len)
        weight = weight_ref[block]
        for position in range(8):
            at = pl.ds(pl.multiple_of(owners_ref[position] * part, part), part)
            total = mine_ref[at, source].astype(F32) + theirs_ref[at, source].astype(F32)
            out_ref[pl.ds(position * part, part), target] = (total * weight).astype(BF)
        return carry

    lax.fori_loop(0, weight_ref.shape[0], one, 0)


def place_rows(mine, theirs, slots, owners, block_weight):
    count, _, block_len = block_weight.shape
    scalars, whole = pl.BlockSpec(memory_space=pltpu.SMEM), pl.BlockSpec(memory_space=pltpu.VMEM)
    return pl.pallas_call(
        place_kernel,
        out_shape=jax.ShapeDtypeStruct((mine.shape[0], count * block_len), BF),
        in_specs=[scalars, scalars, whole, whole, whole],
        out_specs=whole,
        compiler_params=pltpu.CompilerParams(vmem_limit_bytes=24 * 1024 * 1024),
        cost_estimate=pl.CostEstimate(flops=3000000, bytes_accessed=9000000, transcendentals=0),
    )(slots, owners, mine, theirs, block_weight)


def join_kernel(axis, *refs):
    pieces, out_ref = refs[:-1], refs[-1]
    size = pieces[0].shape[axis]
    for place, piece in enumerate(pieces):
        at = pl.ds(place * size, size)
        if axis == 0:
            out_ref[at, :] = piece[...]
        else:
            out_ref[:, at] = piece[...]


def join(pieces, axis):
    shape = list(pieces[0].shape)
    shape[axis] *= len(pieces)
    whole = pl.BlockSpec(memory_space=pltpu.VMEM)
    return pl.pallas_call(
        functools.partial(join_kernel, axis),
        out_shape=jax.ShapeDtypeStruct(tuple(shape), BF),
        in_specs=[whole] * len(pieces),
        out_specs=whole,
        compiler_params=pltpu.CompilerParams(vmem_limit_bytes=16 * 1024 * 1024),
        cost_estimate=pl.CostEstimate(flops=0, bytes_accessed=6500000, transcendentals=0),
    )(*pieces)


Z_RING = ("z", "y_hi")


def body(tokens, assign, gates, cot, w_in, w_out):
    w_in, w_out = w_in[0], w_out[0]
    width, units = w_in.shape
    count = assign.shape[0]
    block_len = tokens.shape[0] // count
    expert = lax.axis_index(OWN).astype(jnp.int32)

    part = cot.shape[1]
    y_at = lax.axis_index("y_lo").astype(jnp.int32)
    position = jnp.arange(8, dtype=jnp.int32)
    owners = ((y_at + position) % 2) * 4 + position // 2

    in_blocks = ring_gather(w_in, side_swap(w_in, Z_RING), Z_RING)
    cot_other = side_swap(cot.T, ("x", "y_lo"))
    cot_side = jnp.concatenate([cot.T, cot_other], 0)
    cot_t = lax.all_gather(cot_side, "x", axis=0, tiled=True)

    is_first, is_second = assign[:, 0] == expert, assign[:, 1] == expert
    hit = jnp.logical_or(is_first, is_second)
    order = jnp.arange(count, dtype=jnp.int32)
    earlier = jnp.logical_and(order[None, :] < order[:, None], hit[None, :])
    rank = jnp.sum(earlier.astype(jnp.int32), axis=1)
    slots = jnp.minimum(rank, CAP - 1)
    slot_ids = jnp.arange(CAP, dtype=jnp.int32)
    match = jnp.logical_and(hit[None, :], rank[None, :] == slot_ids[:, None])
    blocks = jnp.sum(jnp.where(match, order[None, :], 0), axis=1)
    gate_blocks = gates.reshape(count, block_len, 2)
    block_weight = jnp.where(is_first[:, None], gate_blocks[..., 0], 0.0) + jnp.where(
        is_second[:, None], gate_blocks[..., 1], 0.0
    )
    slot_weight = jnp.sum(jnp.where(match[:, :, None], block_weight[None], 0.0), axis=1)
    hit_weight = jnp.broadcast_to(hit.astype(F32)[:, None], (count, block_len))

    half = CAP * block_len
    picked = tokens.reshape(count, block_len, width)[blocks].reshape(half, width)
    rows_other = core_swap(picked)
    rows = lax.optimization_barrier(jnp.concatenate([picked, rows_other], 0))
    full_in = join(in_blocks, 1)
    pre = dot(rows, full_in, ((1,), (0,)))
    act, act_slope = (pre * gelu_cdf(pre)).astype(BF), gelu_slope(pre).astype(BF)
    hidden, slope = lax.optimization_barrier((act, act_slope))

    out_other = y_step_down(y_step_down(w_out))
    out_blocks = ring_gather(w_out, out_other, Z_RING)
    grad_mine = pick_rows(cot_t, blocks, owners, slot_weight[..., None])
    grad_out = lax.optimization_barrier(jnp.concatenate([grad_mine, core_swap(grad_mine)], 0))

    group = 2 * units

    def out_term(k):
        both = dot(hidden[:, k * group : (k + 1) * group], grad_out, ((0,), (0,)))
        return both[:units], both[units:]

    grad_w_out = ring_scatter(out_term(0), out_term(1), out_term(2), out_term(3), Z_RING)

    full_out = join(out_blocks, 0)

    def placed(value, matrix, dims, weight):
        theirs = core_swap(dot(matrix, value[half:], dims).astype(BF))
        mine = dot(matrix, value[:half], dims).astype(BF)
        parts = place_rows(mine, theirs, slots, owners, weight[:, None])
        summed = lax.psum_scatter(parts, "x", scatter_dimension=0, tiled=True)
        other = side_swap(summed[part:], ("x", "y_lo"))
        return plus(summed[:part], other).T

    mixed = placed(hidden, full_out, ((0,), (1,)), block_weight)

    grad_hidden = dot(grad_out, full_out, ((1,), (1,)))
    grad_pre = (grad_hidden * slope.astype(F32)).astype(BF)
    grad_tokens = placed(grad_pre, full_in, ((1,), (1,)), hit_weight)

    def in_term(k):
        both = dot(rows, grad_pre[:, k * group : (k + 1) * group], ((0,), (0,)))
        return both[:, :units], both[:, units:]

    grad_w_in = ring_scatter(in_term(0), in_term(1), in_term(2), in_term(3), Z_RING)
    return mixed, grad_tokens, grad_w_in[None], grad_w_out[None]


def solution(mesh):
    split = Mesh(mesh.devices.reshape(2, 4, 2, 4, 2), OWN + DP)
    return jax.shard_map(
        body,
        mesh=split,
        in_specs=(
            P(DP, None),
            P(DP, None),
            P(DP, None),
            P(DP, OWN),
            P(OWN, None, DP),
            P(OWN, DP, None),
        ),
        out_specs=(P(DP, OWN), P(DP, OWN), P(OWN, None, DP), P(OWN, DP, None)),
        check_vma=False,
    )
```

```python
import functools

import jax
import jax.numpy as jnp
from jax import lax
from jax.experimental import pallas as pl
from jax.experimental.pallas import tpu as pltpu
from jax.sharding import Mesh, PartitionSpec as P


CAP = 5
BF = jnp.bfloat16
F32 = jnp.float32
OWN = ("y_lo", "x")
DP = ("y_hi", "z", "core")


def shift(value, axis, size, step):
    return lax.ppermute(value, axis, [(i, (i + step) % size) for i in range(size)])


def ring_up(value, ring):
    return shift(value, ring[0], 4, 1)


def ring_down(value, ring):
    return shift(value, ring[0], 4, 3)


def side_swap(value, ring):
    return shift(value, ring[1], 2, 1)


def core_swap(value):
    return shift(value, "core", 2, 1)


def y_step_down(value):
    at = [(y % 2) * 2 + y // 2 for y in range(4)]
    return lax.ppermute(value, ("y_lo", "y_hi"), [(at[y], at[(y + 3) % 4]) for y in range(4)])


def ring_gather(block, other, ring):
    below, above = ring_up(block, ring), ring_down(block, ring)
    other_below, other_above = ring_up(other, ring), ring_down(other, ring)
    far, other_far = ring_up(below, ring), ring_down(other_above, ring)
    return [block, other, below, other_below, above, other_above, far, other_far]


def plus(term, got):
    return (term.astype(F32) + got.astype(F32)).astype(BF)


def ring_scatter(near, down, up, far, ring):
    got_up = ring_up(far[0].astype(BF), ring)
    got_down = ring_down(far[1].astype(BF), ring)
    below_other = ring_up(up[1].astype(BF), ring)
    above_this = ring_down(down[0].astype(BF), ring)
    below_this = ring_up(plus(up[0], got_up), ring)
    above_other = ring_down(plus(down[1], got_down), ring)
    other = near[1].astype(F32) + below_other.astype(F32) + above_other.astype(F32)
    this = near[0].astype(F32) + below_this.astype(F32) + above_this.astype(F32)
    return this + side_swap(other.astype(BF), ring).astype(F32)


def gelu_cdf(values):
    return 0.5 * (1.0 + lax.erf(values * 0.7071067811865476))


def gelu_slope(values):
    return gelu_cdf(values) + values * jnp.exp(-0.5 * values * values) * 0.3989422804014327


def dot(a, b, dims):
    return lax.dot_general(a, b, (dims, ((), ())), preferred_element_type=F32)


def pick_kernel(blocks_ref, owners_ref, cot_ref, weight_ref, out_ref, whole_ref):
    part, block_len = cot_ref.shape[0] // 8, weight_ref.shape[1]

    def one(slot, carry):
        source = pl.ds(pl.multiple_of(blocks_ref[slot] * block_len, block_len), block_len)
        for position in range(8):
            at = pl.multiple_of(owners_ref[position] * part, part)
            whole_ref[pl.ds(at, part), :] = cot_ref[pl.ds(position * part, part), source]
        target = pl.ds(pl.multiple_of(slot * block_len, block_len), block_len)
        out_ref[target, :] = (whole_ref[...].T.astype(F32) * weight_ref[slot]).astype(BF)
        return carry

    lax.fori_loop(0, weight_ref.shape[0], one, 0)


def pick_rows(cot_t, blocks, owners, slot_weight):
    width = cot_t.shape[0]
    cap, block_len, _ = slot_weight.shape
    scalars, whole = pl.BlockSpec(memory_space=pltpu.SMEM), pl.BlockSpec(memory_space=pltpu.VMEM)
    return pl.pallas_call(
        pick_kernel,
        out_shape=jax.ShapeDtypeStruct((cap * block_len, width), BF),
        in_specs=[scalars, scalars, whole, whole],
        out_specs=whole,
        scratch_shapes=[pltpu.VMEM((width, block_len), BF)],
        compiler_params=pltpu.CompilerParams(vmem_limit_bytes=16 * 1024 * 1024),
        cost_estimate=pl.CostEstimate(flops=2000000, bytes_accessed=8000000, transcendentals=0),
    )(blocks, owners, cot_t, slot_weight)


def place_kernel(slots_ref, owners_ref, mine_ref, theirs_ref, weight_ref, out_ref):
    part, block_len = out_ref.shape[0] // 8, weight_ref.shape[2]

    def one(block, carry):
        source = pl.ds(pl.multiple_of(slots_ref[block] * block_len, block_len), block_len)
        target = pl.ds(pl.multiple_of(block * block_len, block_len), block_len)
        weight = weight_ref[block]
        for position in range(8):
            at = pl.ds(pl.multiple_of(owners_ref[position] * part, part), part)
            total = mine_ref[at, source].astype(F32) + theirs_ref[at, source].astype(F32)
            out_ref[pl.ds(position * part, part), target] = (total * weight).astype(BF)
        return carry

    lax.fori_loop(0, weight_ref.shape[0], one, 0)


def place_rows(mine, theirs, slots, owners, block_weight):
    count, _, block_len = block_weight.shape
    scalars, whole = pl.BlockSpec(memory_space=pltpu.SMEM), pl.BlockSpec(memory_space=pltpu.VMEM)
    return pl.pallas_call(
        place_kernel,
        out_shape=jax.ShapeDtypeStruct((theirs.shape[0], count * block_len), BF),
        in_specs=[scalars, scalars, whole, whole, whole],
        out_specs=whole,
        compiler_params=pltpu.CompilerParams(vmem_limit_bytes=24 * 1024 * 1024),
        cost_estimate=pl.CostEstimate(flops=3000000, bytes_accessed=9000000, transcendentals=0),
    )(slots, owners, mine, theirs, block_weight)


def join_kernel(axis, *refs):
    pieces, out_ref = refs[:-1], refs[-1]
    size = pieces[0].shape[axis]
    for place, piece in enumerate(pieces):
        at = pl.ds(place * size, size)
        if axis == 0:
            out_ref[at, :] = piece[...]
        else:
            out_ref[:, at] = piece[...]


def join(pieces, axis):
    shape = list(pieces[0].shape)
    shape[axis] *= len(pieces)
    whole = pl.BlockSpec(memory_space=pltpu.VMEM)
    return pl.pallas_call(
        functools.partial(join_kernel, axis),
        out_shape=jax.ShapeDtypeStruct(tuple(shape), BF),
        in_specs=[whole] * len(pieces),
        out_specs=whole,
        compiler_params=pltpu.CompilerParams(vmem_limit_bytes=16 * 1024 * 1024),
        cost_estimate=pl.CostEstimate(flops=0, bytes_accessed=6500000, transcendentals=0),
    )(*pieces)


Z_RING = ("z", "y_hi")


def body(tokens, assign, gates, cot, w_in, w_out):
    w_in, w_out = w_in[0], w_out[0]
    width, units = w_in.shape
    count = assign.shape[0]
    block_len = tokens.shape[0] // count
    expert = lax.axis_index(OWN).astype(jnp.int32)

    part = cot.shape[1]
    y_at = lax.axis_index("y_lo").astype(jnp.int32)
    position = jnp.arange(8, dtype=jnp.int32)
    owners = ((y_at + position) % 2) * 4 + position // 2

    in_blocks = ring_gather(w_in, side_swap(w_in, Z_RING), Z_RING)
    cot_other = side_swap(cot.T, ("x", "y_lo"))
    cot_side = jnp.concatenate([cot.T, cot_other], 0)
    cot_t = lax.all_gather(cot_side, "x", axis=0, tiled=True)

    is_first, is_second = assign[:, 0] == expert, assign[:, 1] == expert
    hit = jnp.logical_or(is_first, is_second)
    order = jnp.arange(count, dtype=jnp.int32)
    earlier = jnp.logical_and(order[None, :] < order[:, None], hit[None, :])
    rank = jnp.sum(earlier.astype(jnp.int32), axis=1)
    slots = jnp.minimum(rank, CAP - 1)
    slot_ids = jnp.arange(CAP, dtype=jnp.int32)
    match = jnp.logical_and(hit[None, :], rank[None, :] == slot_ids[:, None])
    blocks = jnp.sum(jnp.where(match, order[None, :], 0), axis=1)
    gate_blocks = gates.reshape(count, block_len, 2)
    block_weight = jnp.where(is_first[:, None], gate_blocks[..., 0], 0.0) + jnp.where(
        is_second[:, None], gate_blocks[..., 1], 0.0
    )
    slot_weight = jnp.sum(jnp.where(match[:, :, None], block_weight[None], 0.0), axis=1)
    hit_weight = jnp.broadcast_to(hit.astype(F32)[:, None], (count, block_len))

    half = CAP * block_len
    picked = tokens.reshape(count, block_len, width)[blocks].reshape(half, width)
    rows_other = core_swap(picked)
    rows = lax.optimization_barrier(jnp.concatenate([picked, rows_other], 0))
    full_in = join(in_blocks, 1)
    pre = dot(rows, full_in, ((1,), (0,)))
    act, act_slope = (pre * gelu_cdf(pre)).astype(BF), gelu_slope(pre).astype(BF)
    hidden, slope = lax.optimization_barrier((act, act_slope))

    out_other = y_step_down(y_step_down(w_out))
    out_blocks = ring_gather(w_out, out_other, Z_RING)
    grad_mine = pick_rows(cot_t, blocks, owners, slot_weight[..., None])
    grad_out = lax.optimization_barrier(jnp.concatenate([grad_mine, core_swap(grad_mine)], 0))

    group = 2 * units

    def four(terms_of):
        far = terms_of(3 * group, 4 * group)
        most = terms_of(0, 3 * group)
        return [(most[k], most[k + 1]) for k in (0, 2, 4)] + [(far[0], far[1])]

    def out_terms(start, stop):
        both = dot(hidden[:, start:stop], grad_out, ((0,), (0,))).astype(BF)
        return [both[k : k + units] for k in range(0, stop - start, units)]

    grad_w_out = ring_scatter(*four(out_terms), Z_RING)

    full_out = join(out_blocks, 0)

    def placed(value, matrix, dims, weight):
        both = dot(matrix, value, dims).astype(BF)
        theirs = core_swap(both[:, half:])
        parts = place_rows(both, theirs, slots, owners, weight[:, None])
        summed = lax.psum_scatter(parts, "x", scatter_dimension=0, tiled=True)
        other = side_swap(summed[part:], ("x", "y_lo"))
        return plus(summed[:part], other).T

    mixed = placed(hidden, full_out, ((0,), (1,)), block_weight)

    grad_hidden = dot(grad_out, full_out, ((1,), (1,)))
    grad_pre = (grad_hidden * slope.astype(F32)).astype(BF)
    grad_tokens = placed(grad_pre, full_in, ((1,), (1,)), hit_weight)

    def in_terms(start, stop):
        both = dot(rows, grad_pre[:, start:stop], ((0,), (0,))).astype(BF)
        return [both[:, k : k + units] for k in range(0, stop - start, units)]

    grad_w_in = ring_scatter(*four(in_terms), Z_RING)
    return mixed, grad_tokens, grad_w_in[None], grad_w_out[None]


def solution(mesh):
    split = Mesh(mesh.devices.reshape(2, 4, 2, 4, 2), OWN + DP)
    return jax.shard_map(
        body,
        mesh=split,
        in_specs=(
            P(DP, None),
            P(DP, None),
            P(DP, None),
            P(DP, OWN),
            P(OWN, None, DP),
            P(OWN, DP, None),
        ),
        out_specs=(P(DP, OWN), P(DP, OWN), P(OWN, None, DP), P(OWN, DP, None)),
        check_vma=False,
    )
```

```python
import functools

import jax
import jax.numpy as jnp
from jax import lax
from jax.experimental import pallas as pl
from jax.experimental.pallas import tpu as pltpu
from jax.sharding import Mesh, PartitionSpec as P


CAP = 5
BF = jnp.bfloat16
F32 = jnp.float32
OWN = ("y_lo", "x")
DP = ("y_hi", "z", "core")


def shift(value, axis, size, step):
    return lax.ppermute(value, axis, [(i, (i + step) % size) for i in range(size)])


def ring_up(value, ring):
    return shift(value, ring[0], 4, 1)


def ring_down(value, ring):
    return shift(value, ring[0], 4, 3)


def side_swap(value, ring):
    return shift(value, ring[1], 2, 1)


def core_swap(value):
    return shift(value, "core", 2, 1)


def y_step_down(value):
    at = [(y % 2) * 2 + y // 2 for y in range(4)]
    return lax.ppermute(value, ("y_lo", "y_hi"), [(at[y], at[(y + 3) % 4]) for y in range(4)])


def ring_gather(block, other, ring):
    below, above = ring_up(block, ring), ring_down(block, ring)
    other_below, other_above = ring_up(other, ring), ring_down(other, ring)
    far, other_far = ring_up(below, ring), ring_down(other_above, ring)
    return [block, other, below, other_below, above, other_above, far, other_far]


def plus(term, got):
    return (term.astype(F32) + got.astype(F32)).astype(BF)


def ring_scatter(near, down, up, far, ring):
    got_up = ring_up(far[0].astype(BF), ring)
    got_down = ring_down(far[1].astype(BF), ring)
    below_other = ring_up(up[1].astype(BF), ring)
    above_this = ring_down(down[0].astype(BF), ring)
    below_this = ring_up(plus(up[0], got_up), ring)
    above_other = ring_down(plus(down[1], got_down), ring)
    other = near[1].astype(F32) + below_other.astype(F32) + above_other.astype(F32)
    this = near[0].astype(F32) + below_this.astype(F32) + above_this.astype(F32)
    return this + side_swap(other.astype(BF), ring).astype(F32)


def gelu_cdf(values):
    return 0.5 * (1.0 + lax.erf(values * 0.7071067811865476))


def gelu_slope(values):
    return gelu_cdf(values) + values * jnp.exp(-0.5 * values * values) * 0.3989422804014327


def dot(a, b, dims):
    return lax.dot_general(a, b, (dims, ((), ())), preferred_element_type=F32)


def pick_kernel(blocks_ref, owners_ref, cot_ref, weight_ref, out_ref, whole_ref):
    part, block_len = cot_ref.shape[0] // 8, weight_ref.shape[1]

    def one(slot, carry):
        source = pl.ds(pl.multiple_of(blocks_ref[slot] * block_len, block_len), block_len)
        for position in range(8):
            at = pl.multiple_of(owners_ref[position] * part, part)
            whole_ref[pl.ds(at, part), :] = cot_ref[pl.ds(position * part, part), source]
        target = pl.ds(pl.multiple_of(slot * block_len, block_len), block_len)
        out_ref[target, :] = (whole_ref[...].T.astype(F32) * weight_ref[slot]).astype(BF)
        return carry

    lax.fori_loop(0, weight_ref.shape[0], one, 0)


def pick_rows(cot_t, blocks, owners, slot_weight):
    width = cot_t.shape[0]
    cap, block_len, _ = slot_weight.shape
    scalars, whole = pl.BlockSpec(memory_space=pltpu.SMEM), pl.BlockSpec(memory_space=pltpu.VMEM)
    return pl.pallas_call(
        pick_kernel,
        out_shape=jax.ShapeDtypeStruct((cap * block_len, width), BF),
        in_specs=[scalars, scalars, whole, whole],
        out_specs=whole,
        scratch_shapes=[pltpu.VMEM((width, block_len), BF)],
        compiler_params=pltpu.CompilerParams(vmem_limit_bytes=8 * 1024 * 1024),
        cost_estimate=pl.CostEstimate(flops=2000000, bytes_accessed=8000000, transcendentals=0),
    )(blocks, owners, cot_t, slot_weight)


def place_kernel(slots_ref, owners_ref, mine_ref, theirs_ref, weight_ref, out_ref):
    part, block_len = out_ref.shape[0] // 8, weight_ref.shape[2]

    def one(block, carry):
        source = pl.ds(pl.multiple_of(slots_ref[block] * block_len, block_len), block_len)
        target = pl.ds(pl.multiple_of(block * block_len, block_len), block_len)
        weight = weight_ref[block]
        for position in range(8):
            at = pl.ds(pl.multiple_of(owners_ref[position] * part, part), part)
            total = mine_ref[at, source].astype(F32) + theirs_ref[at, source].astype(F32)
            out_ref[pl.ds(position * part, part), target] = (total * weight).astype(BF)
        return carry

    lax.fori_loop(0, weight_ref.shape[0], one, 0)


def place_rows(mine, theirs, slots, owners, block_weight):
    count, _, block_len = block_weight.shape
    scalars, whole = pl.BlockSpec(memory_space=pltpu.SMEM), pl.BlockSpec(memory_space=pltpu.VMEM)
    return pl.pallas_call(
        place_kernel,
        out_shape=jax.ShapeDtypeStruct((theirs.shape[0], count * block_len), BF),
        in_specs=[scalars, scalars, whole, whole, whole],
        out_specs=whole,
        compiler_params=pltpu.CompilerParams(vmem_limit_bytes=12 * 1024 * 1024),
        cost_estimate=pl.CostEstimate(flops=3000000, bytes_accessed=9000000, transcendentals=0),
    )(slots, owners, mine, theirs, block_weight)


def join_kernel(axis, *refs):
    pieces, out_ref = refs[:-1], refs[-1]
    size = pieces[0].shape[axis]
    for place, piece in enumerate(pieces):
        at = pl.ds(place * size, size)
        if axis == 0:
            out_ref[at, :] = piece[...]
        else:
            out_ref[:, at] = piece[...]


def join(pieces, axis):
    shape = list(pieces[0].shape)
    shape[axis] *= len(pieces)
    whole = pl.BlockSpec(memory_space=pltpu.VMEM)
    return pl.pallas_call(
        functools.partial(join_kernel, axis),
        out_shape=jax.ShapeDtypeStruct(tuple(shape), BF),
        in_specs=[whole] * len(pieces),
        out_specs=whole,
        compiler_params=pltpu.CompilerParams(vmem_limit_bytes=8 * 1024 * 1024),
        cost_estimate=pl.CostEstimate(flops=0, bytes_accessed=6500000, transcendentals=0),
    )(*pieces)


Z_RING = ("z", "y_hi")


def body(tokens, assign, gates, cot, w_in, w_out):
    w_in, w_out = w_in[0], w_out[0]
    width, units = w_in.shape
    count = assign.shape[0]
    block_len = tokens.shape[0] // count
    expert = lax.axis_index(OWN).astype(jnp.int32)

    part = cot.shape[1]
    y_at = lax.axis_index("y_lo").astype(jnp.int32)
    position = jnp.arange(8, dtype=jnp.int32)
    owners = ((y_at + position) % 2) * 4 + position // 2

    in_blocks = ring_gather(w_in, side_swap(w_in, Z_RING), Z_RING)
    cot_other = side_swap(cot.T, ("x", "y_lo"))
    cot_side = jnp.concatenate([cot.T, cot_other], 0)
    cot_t = lax.all_gather(cot_side, "x", axis=0, tiled=True)

    is_first, is_second = assign[:, 0] == expert, assign[:, 1] == expert
    hit = jnp.logical_or(is_first, is_second)
    order = jnp.arange(count, dtype=jnp.int32)
    earlier = jnp.logical_and(order[None, :] < order[:, None], hit[None, :])
    rank = jnp.sum(earlier.astype(jnp.int32), axis=1)
    slots = jnp.minimum(rank, CAP - 1)
    slot_ids = jnp.arange(CAP, dtype=jnp.int32)
    match = jnp.logical_and(hit[None, :], rank[None, :] == slot_ids[:, None])
    blocks = jnp.sum(jnp.where(match, order[None, :], 0), axis=1)
    gate_blocks = gates.reshape(count, block_len, 2)
    block_weight = jnp.where(is_first[:, None], gate_blocks[..., 0], 0.0) + jnp.where(
        is_second[:, None], gate_blocks[..., 1], 0.0
    )
    slot_weight = jnp.sum(jnp.where(match[:, :, None], block_weight[None], 0.0), axis=1)
    hit_weight = jnp.broadcast_to(hit.astype(F32)[:, None], (count, block_len))

    half = CAP * block_len
    picked = tokens.reshape(count, block_len, width)[blocks].reshape(half, width)
    rows_other = core_swap(picked)
    rows = lax.optimization_barrier(jnp.concatenate([picked, rows_other], 0))
    full_in = join(in_blocks, 1)
    pre = dot(rows, full_in, ((1,), (0,)))
    act, act_slope = (pre * gelu_cdf(pre)).astype(BF), gelu_slope(pre).astype(BF)
    hidden, slope = lax.optimization_barrier((act, act_slope))

    out_other = y_step_down(y_step_down(w_out))
    out_blocks = ring_gather(w_out, out_other, Z_RING)
    grad_mine = pick_rows(cot_t, blocks, owners, slot_weight[..., None])
    grad_out = lax.optimization_barrier(jnp.concatenate([grad_mine, core_swap(grad_mine)], 0))

    group = 2 * units

    def four(terms_of):
        far = terms_of(3 * group, 4 * group)
        most = terms_of(0, 3 * group)
        return [(most[k], most[k + 1]) for k in (0, 2, 4)] + [(far[0], far[1])]

    def out_terms(start, stop):
        both = dot(hidden[:, start:stop], grad_out, ((0,), (0,))).astype(BF)
        return [both[k : k + units] for k in range(0, stop - start, units)]

    grad_w_out = ring_scatter(*four(out_terms), Z_RING)

    full_out = join(out_blocks, 0)

    def placed(value, matrix, dims, weight):
        both = dot(matrix, value, dims).astype(BF)
        theirs = core_swap(both[:, half:])
        parts = place_rows(both, theirs, slots, owners, weight[:, None])
        summed = lax.psum_scatter(parts, "x", scatter_dimension=0, tiled=True)
        other = side_swap(summed[part:], ("x", "y_lo"))
        return plus(summed[:part], other).T

    mixed = placed(hidden, full_out, ((0,), (1,)), block_weight)

    grad_hidden = dot(grad_out, full_out, ((1,), (1,)))
    grad_pre = (grad_hidden * slope.astype(F32)).astype(BF)
    grad_tokens = placed(grad_pre, full_in, ((1,), (1,)), hit_weight)

    def in_terms(start, stop):
        both = dot(rows, grad_pre[:, start:stop], ((0,), (0,))).astype(BF)
        return [both[:, k : k + units] for k in range(0, stop - start, units)]

    grad_w_in = ring_scatter(*four(in_terms), Z_RING)
    return mixed, grad_tokens, grad_w_in[None], grad_w_out[None]


def solution(mesh):
    split = Mesh(mesh.devices.reshape(2, 4, 2, 4, 2), OWN + DP)
    return jax.shard_map(
        body,
        mesh=split,
        in_specs=(
            P(DP, None),
            P(DP, None),
            P(DP, None),
            P(DP, OWN),
            P(OWN, None, DP),
            P(OWN, DP, None),
        ),
        out_specs=(P(DP, OWN), P(DP, OWN), P(OWN, None, DP), P(OWN, DP, None)),
        check_vma=False,
    )
```
